1024 devices in a mesh: tm: 32 (over y_hi, x, core), height: 4 (over y_lo), fsdp: 8 (over z).
Axes of the slice: x: 8, y: 8 (y_hi: 2, y_lo: 4; y = y_hi * 4 + y_lo), z: 8, core: 2. Of those that a mesh axis runs over, the one named last changes fastest.
Arguments:
- query_primal: bfloat16 [8, 128, 16, 8, 1536], P('fsdp', 'tm', 'height'), may hold values from -125 to 125
- key_primal: bfloat16 [8, 128, 16, 8, 1536], P('fsdp', 'tm', 'height'), may hold values from -5 to 5
- value_primal: bfloat16 [8, 128, 16, 8, 1536], P('fsdp', 'tm', 'height'), may hold values from -6 to 6
- query_tangent: bfloat16 [8, 128, 16, 8, 1536], P('fsdp', 'tm', 'height'), may hold values from -6 to 6
- key_tangent: bfloat16 [8, 128, 16, 8, 1536], P('fsdp', 'tm', 'height'), may hold values from -6 to 6
- value_tangent: bfloat16 [8, 128, 16, 8, 1536], P('fsdp', 'tm', 'height'), may hold values from -6 to 6
- out_weight: bfloat16 [1536, 1536], P(None, ('height', 'fsdp')), may hold values from -0.15625 to 0.15625
- gate_table: float32 [64, 1536], replicated, may hold values from 0.5 to 1.5
- gate_slope: float32 [64, 1536], replicated, may hold values from -4 to 4
- timestep: int32 [8], P('fsdp'), may hold values from 0 to 63
Outputs:
- output_primal: bfloat16 [8, 128, 16, 8, 1536], P('fsdp', 'tm', 'height')
- output_tangent: bfloat16 [8, 128, 16, 8, 1536], P('fsdp', 'tm', 'height')
The draws below stay inside these ranges and needn't reach their ends.
All inputs are finite; a program needn't handle non-finite values.
Results may differ from the reference program's by a relative error of at most 0.008.
Values may be sent and summed in bfloat16 or wider, within the bound.
A program may use at most 64 MiB of HBM per device.

```python
import math
import jax
import jax.numpy as jnp
from jax import lax

HEADS = 12
HD = 128
DOUT = 1536
TF = 4
TR = 8
COLS = 8
STEPS = 64
BATCH = 8
FRAMES = 128
ROWS = 16


def query_key_pair(key):
    dims_all = (BATCH * FRAMES * ROWS * COLS, HEADS * HD)
    queries = jnp.clip(jax.random.normal(jax.random.fold_in(key, 101), dims_all, jnp.float32), -4.0, 4.0)
    key_draw = jnp.clip(jax.random.normal(jax.random.fold_in(key, 102), dims_all, jnp.float32), -4.0, 4.0)
    full = (BATCH, FRAMES, ROWS, COLS, HEADS * HD)
    return (queries.reshape(full), key_draw.reshape(full))


def draw_query_primal(key, part):
    return query_key_pair(key)[0].astype(jnp.bfloat16)


def draw_key_primal(key, part):
    return query_key_pair(key)[1].astype(jnp.bfloat16)


def place_ends(result, rng, least, top_value):
    shape = result.shape
    spot = [jax.random.randint(jax.random.fold_in(rng, axis), (), 0, shape[axis]) for axis in range(len(shape))]
    result = result.at[tuple(spot)].set(least)
    longest = shape.index(max(shape))
    spot[longest] = (spot[longest] + 1) % shape[longest]
    return result.at[tuple(spot)].set(top_value)


def steps_of(stream_key, extent, split, low, high):
    gain = 1.0
    for axis_at, parts in split:
        draws = jax.random.uniform(jax.random.fold_in(jax.random.fold_in(stream_key, 6), axis_at), (parts,), jnp.float32, low / len(split), high / len(split))
        gain = gain * jnp.repeat(jnp.exp(draws), extent[axis_at] // parts).reshape((-1,) + (1,) * (len(extent) - 1 - axis_at))
    return gain


def gaussian(stream_key, shape, deviation, reach, cuts=(), held_as=jnp.bfloat16):
    values = jax.random.normal(stream_key, shape, jnp.float32) * deviation
    if len(cuts) > 0:
        values = steps_of(stream_key, shape, cuts, -0.22, 0.18) * values
    return jnp.clip(values, min=-reach, max=reach).astype(held_as)


def setup_inputs(seed: int = 0) -> dict:
    streams_of = jax.random.split(jax.random.key(seed), 11)
    query_primal = draw_query_primal(jax.random.fold_in(streams_of[10], 71), 0)
    key_primal = draw_key_primal(jax.random.fold_in(streams_of[10], 71), 0)
    value_primal = gaussian(streams_of[2], (BATCH, FRAMES, ROWS, COLS, HEADS * HD), 1.0, 6.0, ((0, 8), (1, 32), (2, 4)))
    query_tangent = gaussian(streams_of[3], (BATCH, FRAMES, ROWS, COLS, HEADS * HD), 1.0, 6.0, ((0, 8), (1, 32), (2, 4)))
    key_tangent = gaussian(streams_of[4], (BATCH, FRAMES, ROWS, COLS, HEADS * HD), 1.0, 6.0, ((0, 8), (1, 32), (2, 4)))
    value_tangent = gaussian(streams_of[5], (BATCH, FRAMES, ROWS, COLS, HEADS * HD), 1.0, 6.0, ((0, 8), (1, 32), (2, 4)))
    out_weight = gaussian(streams_of[6], (HEADS * HD, DOUT), (HEADS * HD) ** -0.5, 0.15625, ((1, 32),))
    gate_table = jnp.clip(jax.random.uniform(streams_of[7], (STEPS, DOUT), jnp.float32, 0.5, 1.5), 0.5, 1.5)
    gate_slope = gaussian(streams_of[8], (STEPS, DOUT), 1.0, 4.0, (), jnp.float32)
    timestep = place_ends(jax.random.randint(streams_of[9], (BATCH,), 0, STEPS), jax.random.fold_in(streams_of[9], 1), 0, STEPS - 1).astype(jnp.int32)
    return {"query_primal": query_primal, "key_primal": key_primal, "value_primal": value_primal, "query_tangent": query_tangent, "key_tangent": key_tangent, "value_tangent": value_tangent, "out_weight": out_weight, "gate_table": gate_table, "gate_slope": gate_slope, "timestep": timestep}


def attend(queries, keys_all, values_all, queries_t, keys_t, values_t, allowed):
    scaling = 1.0 / math.sqrt(queries.shape[-1])
    query_f = queries.astype(jnp.float32)
    key_f = keys_all.astype(jnp.float32)
    scores = jnp.einsum('qhd,khd->hqk', query_f, key_f) * scaling
    scores = jnp.where(allowed[None], scores, -1e+30)
    row_max = lax.optimization_barrier(jnp.max(scores, axis=-1, keepdims=True))
    lifted = jnp.exp(scores - row_max)
    probs = lifted / lax.optimization_barrier(jnp.sum(lifted, axis=-1, keepdims=True))
    probs_low = probs.astype(jnp.bfloat16)
    primal = jnp.einsum('hqk,khd->qhd', probs_low.astype(jnp.float32), values_all.astype(jnp.float32))
    slopes = (jnp.einsum('qhd,khd->hqk', queries_t.astype(jnp.float32), key_f) + jnp.einsum('qhd,khd->hqk', query_f, keys_t.astype(jnp.float32))) * scaling
    centre = lax.optimization_barrier(jnp.sum(probs * slopes, axis=-1, keepdims=True))
    weights_t = (probs * (slopes - centre)).astype(jnp.bfloat16)
    tangent = jnp.einsum('hqk,khd->qhd', weights_t.astype(jnp.float32), values_all.astype(jnp.float32)) + jnp.einsum('hqk,khd->qhd', probs_low.astype(jnp.float32), values_t.astype(jnp.float32))
    return (primal.astype(jnp.bfloat16), tangent.astype(jnp.bfloat16))

def reference(query_primal, key_primal, value_primal, query_tangent, key_tangent, value_tangent, out_weight, gate_table, gate_slope, timestep):
    batches, frames, rows, columns, features = query_primal.shape
    head_count = features // HD
    time_tiles = frames // TF
    row_tiles = rows // TR
    widths = ((0, 0), (1, 1), (0, 0), (0, 0), (0, 0))
    padded = [jnp.pad(array, widths) for array in (key_primal, value_primal, key_tangent, value_tangent)]
    ext_frames = TF + 2
    frame_ids = lax.broadcasted_iota(jnp.int32, (ext_frames, TR, columns), 0).reshape(-1)
    zero_idx = jnp.zeros((), jnp.int32)

    def one_tile(tile_id):
        batch_id = (tile_id // (time_tiles * row_tiles)).astype(jnp.int32)
        time_id = (tile_id // row_tiles % time_tiles).astype(jnp.int32)
        row_id = (tile_id % row_tiles).astype(jnp.int32)
        first_frame = (time_id * TF).astype(jnp.int32)
        first_row = (row_id * TR).astype(jnp.int32)

        def cut(array, length):
            block = lax.dynamic_slice(array, (batch_id, first_frame, first_row, zero_idx, zero_idx), (1, length, TR, columns, features))
            return block.reshape(-1, head_count, HD)
        global_frame = first_frame + frame_ids - 1
        inside = (global_frame >= 0) & (global_frame < frames)
        allowed = inside[None, :]
        primal, tangent = attend(cut(query_primal, TF), cut(padded[0], ext_frames), cut(padded[1], ext_frames), cut(query_tangent, TF), cut(padded[2], ext_frames), cut(padded[3], ext_frames), allowed)
        return (primal.reshape(TF, TR, columns, features), tangent.reshape(TF, TR, columns, features))
    tile_total = batches * time_tiles * row_tiles
    primal_tiles, tangent_tiles = lax.map(one_tile, jnp.arange(tile_total, dtype=jnp.int32))

    def arrange(tiles):
        tiles = tiles.reshape(batches, time_tiles, row_tiles, TF, TR, columns, features)
        return tiles.transpose(0, 1, 3, 2, 4, 5, 6).reshape(batches, frames, rows, columns, features)
    attn_primal = arrange(primal_tiles)
    attn_tangent = arrange(tangent_tiles)

    def project_batch(batch_id):
        flat_p = lax.dynamic_index_in_dim(attn_primal, batch_id, 0, keepdims=False).reshape(-1, features)
        flat_t = lax.dynamic_index_in_dim(attn_tangent, batch_id, 0, keepdims=False).reshape(-1, features)
        projected = jnp.dot(flat_p, out_weight, preferred_element_type=jnp.float32)
        projected_t = jnp.dot(flat_t, out_weight, preferred_element_type=jnp.float32)
        step_id = lax.dynamic_index_in_dim(timestep, batch_id, 0, keepdims=False).astype(jnp.int32)
        gate_row = lax.dynamic_index_in_dim(gate_table, step_id, 0, keepdims=False)
        slope_row = lax.dynamic_index_in_dim(gate_slope, step_id, 0, keepdims=False)
        out_p = (gate_row * projected).astype(jnp.bfloat16)
        out_t = (gate_row * projected_t + slope_row * projected).astype(jnp.bfloat16)
        return (out_p, out_t)
    outs_p, outs_t = lax.map(project_batch, jnp.arange(batches, dtype=jnp.int32))
    dout = out_weight.shape[1]
    return (outs_p.reshape(batches, frames, rows, columns, dout), outs_t.reshape(batches, frames, rows, columns, dout))
```

```python
import functools
import math

import jax
import jax.numpy as jnp
from jax import lax
from jax.experimental import pallas as pl
from jax.experimental.pallas import tpu as pltpu
from jax.sharding import PartitionSpec as P

HD = 128
PAIR = 2
MESH = pl.DeviceIdType.MESH
NT = (((1,), (1,)), ((), ()))


def kernel(
    dims,
    step_ref,
    q_ref,
    k_ref,
    v_ref,
    qt_ref,
    kt_ref,
    vt_ref,
    w_ref,
    gate_ref,
    slope_ref,
    outp_ref,
    outt_ref,
    kv,
    qq,
    attn,
    wbuf,
    gates,
    load_sem,
    part_s,
    part_r,
    ownl_s,
    ownl_r,
    ownr_s,
    ownr_r,
    rell_s,
    rell_r,
    relr_s,
    relr_r,
    ws,
    wr,
):
    n_tm, n_h, n_z, tokens, frame, features, shard = dims
    chunks = features // (PAIR * HD)
    wide = PAIR * HD
    khalf = features // 2
    half_tm = n_tm // 2
    tm = lax.axis_index("tm")
    h = lax.axis_index("height")
    z = lax.axis_index("fsdp")
    core = lax.rem(tm, 2)
    twin = h + 1 - 2 * lax.rem(h, 2)
    partner = (tm, twin, z)
    outer = jnp.logical_or(h == 0, h == n_h - 1)
    gap = (jnp.where(outer, lax.rem(tm + half_tm, n_tm), tm), n_h - 1 - h, z)
    z_up = lax.rem(z + 1, n_z)
    z_down = lax.rem(z + n_z - 1, n_z)
    above = (tm, h, z_up)
    below = (tm, h, z_down)
    left = (tm - 1, h, z)
    right = (tm + 1, h, z)
    sibling = (tm + 1 - 2 * core, h, z)
    has_left = tm > 0
    has_right = tm < n_tm - 1
    cross_left = tm == half_tm
    cross_right = tm == half_tm - 1

    own = 0
    other = tokens
    left_own = 2 * tokens
    left_other = left_own + frame
    right_own = left_other + frame
    right_other = right_own + frame
    last = tokens - frame

    barrier = pltpu.get_barrier_semaphore()
    for peer in (partner, gap, above, below):
        pl.semaphore_signal(barrier, inc=1, device_id=peer, device_id_type=MESH)

    @pl.when(has_left)
    def _():
        pl.semaphore_signal(barrier, inc=1, device_id=left, device_id_type=MESH)

    @pl.when(has_right)
    def _():
        pl.semaphore_signal(barrier, inc=1, device_id=right, device_id_type=MESH)

    kv_loads = [
        pltpu.make_async_copy(ref, kv.at[i, pl.ds(own, tokens)], load_sem.at[i])
        for i, ref in enumerate((k_ref, v_ref, kt_ref, vt_ref))
    ]
    q_loads = [
        pltpu.make_async_copy(ref, qq.at[i], load_sem.at[4 + i])
        for i, ref in enumerate((q_ref, qt_ref))
    ]
    gate_loads = [
        pltpu.make_async_copy(ref, gates.at[i], load_sem.at[6 + i])
        for i, ref in enumerate((gate_ref, slope_ref))
    ]
    columns = pl.ds(pl.multiple_of(core * khalf, HD), khalf)

    def shard_of(height):
        return wbuf.at[core, z, pl.ds(pl.multiple_of(height * shard, 16), shard)]

    w_load = pltpu.make_async_copy(w_ref.at[:, columns], shard_of(h), load_sem.at[8])
    w_load.start()
    for copy in kv_loads + q_loads + gate_loads:
        copy.start()

    rows = 2 * frame

    @pl.when(jnp.logical_not(has_left))
    def _():
        kv[:, pl.ds(left_own, rows), :] = jnp.zeros((4, rows, features), kv.dtype)

    @pl.when(jnp.logical_not(has_right))
    def _():
        kv[:, pl.ds(right_own, rows), :] = jnp.zeros((4, rows, features), kv.dtype)

    w_load.wait()
    for copy in kv_loads:
        copy.wait()
    peers = 4 + has_left.astype(jnp.int32) + has_right.astype(jnp.int32)
    pl.semaphore_wait(barrier, peers)

    def move(source, target, send, recv, device):
        return pltpu.make_async_remote_copy(
            src_ref=source,
            dst_ref=target,
            send_sem=send,
            recv_sem=recv,
            device_id=device,
            device_id_type=MESH,
        )

    def block(row, count, g):
        cols = pl.ds(pl.multiple_of(g * wide, wide), wide)
        return kv.at[:, pl.ds(row, count), cols]

    def to_partner(g):
        return move(block(own, tokens, g), block(other, tokens, g), part_s.at[g], part_r.at[g], partner)

    def own_left(g):
        return move(block(own, frame, g), block(right_own, frame, g), ownl_s.at[g], ownr_r.at[g], left)

    def own_right(g):
        return move(block(last, frame, g), block(left_own, frame, g), ownr_s.at[g], ownl_r.at[g], right)

    def relay_left(g):
        return move(block(other, frame, g), block(right_other, frame, g), rell_s.at[g], relr_r.at[g], left)

    def relay_right(g):
        return move(block(other + last, frame, g), block(left_other, frame, g), relr_s.at[g], rell_r.at[g], right)

    def cross_to_left(g):
        return move(block(left_own, frame, g), block(left_other, frame, g), rell_s.at[g], rell_r.at[g], partner)

    def cross_to_right(g):
        return move(block(right_own, frame, g), block(right_other, frame, g), relr_s.at[g], relr_r.at[g], partner)

    def shard_move(height, slot, device):
        return move(shard_of(height), shard_of(height), ws.at[slot], wr.at[slot], device)

    to_p = shard_move(h, 0, partner)
    to_g = shard_move(h, 1, gap)
    on_g = shard_move(twin, 2, gap)

    def z_block(which, parts):
        block_rows = n_h * shard
        first, count = (0, block_rows)
        if parts == 1:
            count = block_rows // 2
        if parts == 2:
            first = count = block_rows // 2
        return wbuf.at[core, which, pl.ds(first, count)]

    hops = n_z // 2

    def ring_up(step):
        ref = z_block(lax.rem(z + n_z - step, n_z), 1 if step == hops - 1 else 0)
        return move(ref, ref, ws.at[3 + step], wr.at[3 + step], above)

    def ring_down(step):
        ref = z_block(lax.rem(z + step, n_z), 2 if step == hops - 1 else 0)
        return move(ref, ref, ws.at[3 + hops + step], wr.at[3 + hops + step], below)

    def across(offset):
        ref = wbuf.at[core, lax.rem(z + offset, n_z)]
        slot = 3 + 2 * hops + offset
        return move(ref, ref, ws.at[slot], wr.at[slot], sibling)

    to_p.start()
    to_g.start()
    to_partner(0).start()
    to_partner(1).start()

    def send_own(g, carry):
        @pl.when(has_left)
        def _():
            own_left(g).start()

        @pl.when(has_right)
        def _():
            own_right(g).start()

        return carry

    lax.fori_loop(0, chunks, send_own, 0)

    to_p.wait_recv()
    on_g.start()
    to_g.wait_recv()
    on_g.wait_recv()
    ring_up(0).start()
    ring_down(0).start()
    across(0).start()

    for copy in q_loads:
        copy.wait()

    scaling = 1.0 / math.sqrt(HD)
    spot = lax.broadcasted_iota(jnp.int32, (1, 4 * frame), 1)
    hidden = jnp.logical_or(
        jnp.logical_and(jnp.logical_not(has_left), spot < 2 * frame),
        jnp.logical_and(jnp.logical_not(has_right), spot >= 2 * frame),
    )
    bias = jnp.where(hidden, -1e30, 0.0).astype(jnp.float32)

    def attend(cols):
        q, qt = qq[0, :, cols], qq[1, :, cols]
        k, v, kt, vt = (kv[i, :, cols] for i in range(4))
        scores = lax.dot_general(q, k, NT, preferred_element_type=jnp.float32) * scaling
        scores = jnp.concatenate([scores[:, : 2 * tokens], scores[:, 2 * tokens :] + bias], 1)
        lifted = jnp.exp(scores - jnp.max(scores, axis=-1, keepdims=True))
        probs = lifted * (1.0 / jnp.sum(lifted, axis=-1, keepdims=True))
        low = probs.astype(jnp.bfloat16)
        slopes = (
            lax.dot_general(
                jnp.concatenate([qt, q], 1),
                jnp.concatenate([k, kt], 1),
                NT,
                preferred_element_type=jnp.float32,
            )
            * scaling
        )
        centre = jnp.sum(probs * slopes, axis=-1, keepdims=True)
        bent = (probs * (slopes - centre)).astype(jnp.bfloat16)
        primal = jnp.dot(low, v, preferred_element_type=jnp.float32)
        tangent = jnp.dot(bent, v, preferred_element_type=jnp.float32)
        tangent = tangent + jnp.dot(low, vt, preferred_element_type=jnp.float32)
        attn[pl.ds(0, tokens), cols] = primal.astype(jnp.bfloat16)
        attn[pl.ds(tokens, tokens), cols] = tangent.astype(jnp.bfloat16)

    def ring_stage(step):
        ring_up(step - 1).wait_recv()
        ring_down(step - 1).wait_recv()
        if step < hops:
            ring_up(step).start()
            ring_down(step).start()
            across(n_z - step).start()
            across(step).start()
        else:
            across(hops).start()

    def chunk(g, carry):
        to_partner(g).wait_recv()

        @pl.when(jnp.logical_and(has_left, jnp.logical_not(cross_left)))
        def _():
            relay_left(g).start()

        @pl.when(jnp.logical_and(has_right, jnp.logical_not(cross_right)))
        def _():
            relay_right(g).start()

        @pl.when(g < chunks - 2)
        def _():
            to_partner(g + 2).start()

        for step in range(1, hops + 1):

            @pl.when(g == step)
            def _():
                ring_stage(step)

        @pl.when(has_left)
        def _():
            own_right(g).wait_recv()

        @pl.when(cross_left)
        def _():
            cross_to_left(g).start()

        @pl.when(has_right)
        def _():
            own_left(g).wait_recv()

        @pl.when(cross_right)
        def _():
            cross_to_right(g).start()

        @pl.when(has_left)
        def _():
            relay_right(g).wait_recv()

        @pl.when(has_right)
        def _():
            relay_left(g).wait_recv()

        for head in range(PAIR):
            attend(pl.ds(pl.multiple_of(g * wide + head * HD, HD), HD))
        return carry

    lax.fori_loop(0, chunks, chunk, 0)

    for copy in gate_loads:
        copy.wait()
    for offset in range(n_z):
        across(offset).wait_recv()

    which = step_ref[0]
    gate_row = gates[0, pl.ds(which, 1), :]
    slope_row = gates[1, pl.ds(which, 1), :]
    span = n_z * shard
    for height in range(n_h):
        outs = slice(height * span, (height + 1) * span)
        both = None
        for part in range(2):
            weight = jnp.concatenate(
                [wbuf[part, i, height * shard : (height + 1) * shard, :] for i in range(n_z)], 0
            )
            term = lax.dot_general(
                attn[:, part * khalf : (part + 1) * khalf],
                weight,
                NT,
                preferred_element_type=jnp.float32,
            )
            both = term if both is None else both + term
        gate = gate_row[:, outs]
        outp_ref[:, outs] = (gate * both[:tokens]).astype(outp_ref.dtype)
        tangent = gate * both[tokens:] + slope_row[:, outs] * both[:tokens]
        outt_ref[:, outs] = tangent.astype(outt_ref.dtype)

    def finish(g, carry):
        to_partner(g).wait_send()

        @pl.when(has_left)
        def _():
            own_left(g).wait_send()
            relay_left(g).wait_send()

        @pl.when(has_right)
        def _():
            own_right(g).wait_send()
            relay_right(g).wait_send()

        return carry

    lax.fori_loop(0, chunks, finish, 0)
    to_p.wait_send()
    to_g.wait_send()
    on_g.wait_send()
    for step in range(hops):
        ring_up(step).wait_send()
        ring_down(step).wait_send()
    for offset in range(n_z):
        across(offset).wait_send()


def local(sizes, q, k, v, qt, kt, vt, weight, gate_table, gate_slope, timestep):
    _, frames, rows, cols, features = q.shape
    tokens = frames * rows * cols
    frame = rows * cols
    shard = weight.shape[1]
    n_tm, n_h, n_z = sizes
    chunks = features // (PAIR * HD)
    flat = [a.reshape(tokens, features) for a in (q, k, v, qt, kt, vt)]
    steps = gate_table.shape[0]
    dma = pltpu.SemaphoreType.DMA
    dims = (n_tm, n_h, n_z, tokens, frame, features, shard)
    weights = 3 + n_z + n_z
    anywhere = pl.BlockSpec(memory_space=pl.ANY)
    out = jax.ShapeDtypeStruct((tokens, features), jnp.bfloat16)
    out_p, out_t = pl.pallas_call(
        functools.partial(kernel, dims),
        out_shape=(out, out),
        in_specs=[pl.BlockSpec(memory_space=pltpu.SMEM)] + [anywhere] * 9,
        out_specs=(pl.BlockSpec(memory_space=pltpu.VMEM),) * 2,
        scratch_shapes=[
            pltpu.VMEM((4, 2 * tokens + 4 * frame, features), jnp.bfloat16),
            pltpu.VMEM((2, tokens, features), jnp.bfloat16),
            pltpu.VMEM((2 * tokens, features), jnp.bfloat16),
            pltpu.VMEM((2, n_z, n_h * shard, features // 2), jnp.bfloat16),
            pltpu.VMEM((2, steps, features), jnp.float32),
            dma((9,)),
        ]
        + [dma((chunks,))] * 10
        + [dma((weights,))] * 2,
        compiler_params=pltpu.CompilerParams(collective_id=0, has_side_effects=True),
        name="tiled_attention",
    )(timestep, *flat, weight.T, gate_table, gate_slope)
    return (out_p.reshape(q.shape), out_t.reshape(q.shape))


def solution(mesh):
    spec = P("fsdp", "tm", "height", None, None)
    in_specs = (spec,) * 6 + (P(None, ("height", "fsdp")), P(None, None), P(None, None), P("fsdp"))
    sizes = (mesh.shape["tm"], mesh.shape["height"], mesh.shape["fsdp"])
    return jax.shard_map(
        functools.partial(local, sizes),
        mesh=mesh,
        in_specs=in_specs,
        out_specs=(spec, spec),
        check_vma=False,
    )
```

```python
import functools
import math

import jax
import jax.numpy as jnp
from jax import lax
from jax.experimental import pallas as pl
from jax.experimental.pallas import tpu as pltpu
from jax.sharding import PartitionSpec as P

HD = 128
PAIR = 2
MESH = pl.DeviceIdType.MESH
NT = (((1,), (1,)), ((), ()))


def kernel(
    dims,
    step_ref,
    q_ref,
    k_ref,
    v_ref,
    qt_ref,
    kt_ref,
    vt_ref,
    w_ref,
    gate_ref,
    slope_ref,
    outp_ref,
    outt_ref,
    kv,
    qq,
    attn,
    wbuf,
    gates,
    step_now,
    hello,
    load_sem,
    part_s,
    part_r,
    ownl_s,
    ownl_r,
    ownr_s,
    ownr_r,
    rell_s,
    rell_r,
    relr_s,
    relr_r,
    ws,
    wr,
):
    n_tm, n_h, n_z, tokens, frame, features, shard = dims
    chunks = features // (PAIR * HD)
    wide = PAIR * HD
    khalf = features // 2
    half_tm = n_tm // 2
    tm = lax.axis_index("tm")
    h = lax.axis_index("height")
    z = lax.axis_index("fsdp")
    core = lax.rem(tm, 2)
    twin = h + 1 - 2 * lax.rem(h, 2)
    partner = (tm, twin, z)
    outer = jnp.logical_or(h == 0, h == n_h - 1)
    gap = (jnp.where(outer, lax.rem(tm + half_tm, n_tm), tm), n_h - 1 - h, z)
    z_up = lax.rem(z + 1, n_z)
    z_down = lax.rem(z + n_z - 1, n_z)
    above = (tm, h, z_up)
    below = (tm, h, z_down)
    left = (tm - 1, h, z)
    right = (tm + 1, h, z)
    sibling = (tm + 1 - 2 * core, h, z)
    has_left = tm > 0
    has_right = tm < n_tm - 1
    cross_left = tm == half_tm
    cross_right = tm == half_tm - 1

    own = 0
    other = tokens
    left_own = 2 * tokens
    left_other = left_own + frame
    right_own = left_other + frame
    right_other = right_own + frame
    last = tokens - frame

    even = lax.rem(tm + h + z, 2) == 0
    odd = jnp.logical_not(even)
    barrier = pltpu.get_barrier_semaphore()

    def greet(semaphore):
        for peer in (partner, gap):
            pl.semaphore_signal(semaphore, inc=1, device_id=peer, device_id_type=MESH)

        @pl.when(has_left)
        def _():
            pl.semaphore_signal(semaphore, inc=1, device_id=left, device_id_type=MESH)

        @pl.when(has_right)
        def _():
            pl.semaphore_signal(semaphore, inc=1, device_id=right, device_id_type=MESH)

    def greet_z(semaphore):
        for peer in (above, below):
            pl.semaphore_signal(semaphore, inc=1, device_id=peer, device_id_type=MESH)

    @pl.when(even)
    def _():
        greet(barrier)

    @pl.when(odd)
    def _():
        greet_z(barrier)

    kv_loads = [
        pltpu.make_async_copy(ref, kv.at[i, pl.ds(own, tokens)], load_sem.at[i])
        for i, ref in enumerate((k_ref, v_ref, kt_ref, vt_ref))
    ]
    q_loads = [
        pltpu.make_async_copy(ref, qq.at[i], load_sem.at[4 + i])
        for i, ref in enumerate((q_ref, qt_ref))
    ]
    gate_loads = [
        pltpu.make_async_copy(ref, gates.at[i], load_sem.at[6 + i])
        for i, ref in enumerate((gate_ref, slope_ref))
    ]
    columns = pl.ds(pl.multiple_of(core * khalf, HD), khalf)

    def shard_of(height):
        return wbuf.at[core, z, pl.ds(pl.multiple_of(height * shard, 16), shard)]

    w_load = pltpu.make_async_copy(w_ref.at[:, columns], shard_of(h), load_sem.at[8])
    step_load = pltpu.make_async_copy(step_ref, step_now, load_sem.at[9])
    w_load.start()
    for copy in kv_loads + q_loads + gate_loads + [step_load]:
        copy.start()

    rows = 2 * frame

    @pl.when(jnp.logical_not(has_left))
    def _():
        kv[:, pl.ds(left_own, rows), :] = jnp.zeros((4, rows, features), kv.dtype)

    @pl.when(jnp.logical_not(has_right))
    def _():
        kv[:, pl.ds(right_own, rows), :] = jnp.zeros((4, rows, features), kv.dtype)

    peers = 2 + has_left.astype(jnp.int32) + has_right.astype(jnp.int32)

    @pl.when(odd)
    def _():
        pl.semaphore_wait(barrier, peers)
        greet(hello.at[0])

    @pl.when(even)
    def _():
        pl.semaphore_wait(hello.at[0], peers)

    w_load.wait()
    for copy in kv_loads:
        copy.wait()

    def move(source, target, send, recv, device):
        return pltpu.make_async_remote_copy(
            src_ref=source,
            dst_ref=target,
            send_sem=send,
            recv_sem=recv,
            device_id=device,
            device_id_type=MESH,
        )

    def block(row, count, g):
        cols = pl.ds(pl.multiple_of(g * wide, wide), wide)
        return kv.at[:, pl.ds(row, count), cols]

    def to_partner(g):
        return move(block(own, tokens, g), block(other, tokens, g), part_s.at[g], part_r.at[g], partner)

    def own_left(g):
        return move(block(own, frame, g), block(right_own, frame, g), ownl_s.at[g], ownr_r.at[g], left)

    def own_right(g):
        return move(block(last, frame, g), block(left_own, frame, g), ownr_s.at[g], ownl_r.at[g], right)

    def relay_left(g):
        return move(block(other, frame, g), block(right_other, frame, g), rell_s.at[g], relr_r.at[g], left)

    def relay_right(g):
        return move(block(other + last, frame, g), block(left_other, frame, g), relr_s.at[g], rell_r.at[g], right)

    def cross_to_left(g):
        return move(block(left_own, frame, g), block(left_other, frame, g), rell_s.at[g], rell_r.at[g], partner)

    def cross_to_right(g):
        return move(block(right_own, frame, g), block(right_other, frame, g), relr_s.at[g], relr_r.at[g], partner)

    def shard_move(height, slot, device):
        return move(shard_of(height), shard_of(height), ws.at[slot], wr.at[slot], device)

    to_p = shard_move(h, 0, partner)
    to_g = shard_move(h, 1, gap)
    on_g = shard_move(twin, 2, gap)

    hops = n_z // 2
    half_rows = n_h * shard // 2

    pair_row = pl.multiple_of(lax.div(h, 2) * half_rows, 16)
    far_row = pl.multiple_of(half_rows - lax.div(h, 2) * half_rows, 16)

    def z_block(which, sub):
        return wbuf.at[core, which, pl.ds(far_row if sub else pair_row, half_rows)]

    def ring_up(step, sub):
        ref = z_block(lax.rem(z + n_z - step, n_z), sub)
        slot = 3 + 2 * step + sub
        return move(ref, ref, ws.at[slot], wr.at[slot], above)

    def ring_down(step, sub):
        ref = z_block(lax.rem(z + step, n_z), sub)
        slot = 3 + 2 * hops + 2 * step + sub
        return move(ref, ref, ws.at[slot], wr.at[slot], below)

    def across(offset):
        ref = wbuf.at[core, lax.rem(z + offset, n_z)]
        slot = 3 + 4 * hops + offset
        return move(ref, ref, ws.at[slot], wr.at[slot], sibling)

    ahead = 3
    to_p.start()
    to_g.start()
    for g in range(ahead):
        to_partner(g).start()

    def send_own(g, carry):
        @pl.when(has_left)
        def _():
            own_left(g).start()

        @pl.when(has_right)
        def _():
            own_right(g).start()

        return carry

    lax.fori_loop(0, chunks, send_own, 0)

    to_p.wait_recv()
    on_g.start()

    @pl.when(even)
    def _():
        pl.semaphore_wait(barrier, 2)
        greet_z(hello.at[1])

    @pl.when(odd)
    def _():
        pl.semaphore_wait(hello.at[1], 2)

    ring_up(0, 0).start()
    ring_down(0, 0).start()

    for copy in q_loads:
        copy.wait()

    scaling = 1.0 / math.sqrt(HD)
    spot = lax.broadcasted_iota(jnp.int32, (1, 4 * frame), 1)
    hidden = jnp.logical_or(
        jnp.logical_and(jnp.logical_not(has_left), spot < 2 * frame),
        jnp.logical_and(jnp.logical_not(has_right), spot >= 2 * frame),
    )
    bias = jnp.where(hidden, -1e30, 0.0).astype(jnp.float32)

    def attend(cols):
        q, qt = qq[0, :, cols], qq[1, :, cols]
        k, v, kt, vt = (kv[i, :, cols] for i in range(4))
        scores = lax.dot_general(q, k, NT, preferred_element_type=jnp.float32) * scaling
        scores = jnp.concatenate([scores[:, : 2 * tokens], scores[:, 2 * tokens :] + bias], 1)
        lifted = jnp.exp(scores - jnp.max(scores, axis=-1, keepdims=True))
        probs = lifted * (1.0 / jnp.sum(lifted, axis=-1, keepdims=True))
        low = probs.astype(jnp.bfloat16)
        slopes = (
            lax.dot_general(
                jnp.concatenate([qt, q], 1),
                jnp.concatenate([k, kt], 1),
                NT,
                preferred_element_type=jnp.float32,
            )
            * scaling
        )
        centre = jnp.sum(probs * slopes, axis=-1, keepdims=True)
        bent = (probs * (slopes - centre)).astype(jnp.bfloat16)
        primal = jnp.dot(low, v, preferred_element_type=jnp.float32)
        tangent = jnp.dot(bent, v, preferred_element_type=jnp.float32)
        tangent = tangent + jnp.dot(low, vt, preferred_element_type=jnp.float32)
        attn[pl.ds(0, tokens), cols] = primal.astype(jnp.bfloat16)
        attn[pl.ds(tokens, tokens), cols] = tangent.astype(jnp.bfloat16)

    def ring_pass(step, sub):
        ups = step < hops or sub == 0
        downs = step < hops or sub == 1
        if ups:
            ring_up(step - 1, sub).wait_recv()
        if downs:
            ring_down(step - 1, sub).wait_recv()
        if step < hops - 1 or (step == hops - 1 and sub == 0):
            ring_up(step, sub).start()
        if step < hops - 1 or (step == hops - 1 and sub == 1):
            ring_down(step, sub).start()

    def ring_stage(g):
        if g == 0:
            to_g.wait_recv()
            on_g.wait_recv()
            ring_up(0, 1).start()
            ring_down(0, 1).start()
            across(0).start()
        if 1 <= g <= hops:
            ring_pass(g, 1)
            if g < hops:
                across(n_z - g).start()
                across(g).start()
            else:
                across(hops).start()
        if g < hops:
            ring_pass(g + 1, 0)

    def forward(g):
        to_partner(g).wait_recv()

        @pl.when(jnp.logical_and(has_left, jnp.logical_not(cross_left)))
        def _():
            relay_left(g).start()

        @pl.when(jnp.logical_and(has_right, jnp.logical_not(cross_right)))
        def _():
            relay_right(g).start()

        early = chunks // 2

        @pl.when(g < 2)
        def _():
            for k in range(early):
                other_chunk = g * early + k

                @pl.when(cross_left)
                def _():
                    own_right(other_chunk).wait_recv()
                    cross_to_left(other_chunk).start()

                @pl.when(cross_right)
                def _():
                    own_left(other_chunk).wait_recv()
                    cross_to_right(other_chunk).start()

        @pl.when(g == 0)
        def _():
            for k in range(ahead, chunks - 1):
                to_partner(k).start()

        @pl.when(g == 1)
        def _():
            to_partner(chunks - 1).start()

    def compute(g):
        @pl.when(jnp.logical_and(has_left, jnp.logical_not(cross_left)))
        def _():
            own_right(g).wait_recv()

        @pl.when(jnp.logical_and(has_right, jnp.logical_not(cross_right)))
        def _():
            own_left(g).wait_recv()

        @pl.when(has_left)
        def _():
            relay_right(g).wait_recv()

        @pl.when(has_right)
        def _():
            relay_left(g).wait_recv()

        for head in range(PAIR):
            attend(pl.ds(pl.multiple_of(g * wide + head * HD, HD), HD))

    def chunk(g, carry):
        @pl.when(g < chunks)
        def _():
            forward(g)

        for stage in range(hops + 1):

            @pl.when(g == stage)
            def _():
                ring_stage(stage)

        @pl.when(g >= 1)
        def _():
            compute(g - 1)

        return carry

    lax.fori_loop(0, chunks + 1, chunk, 0)

    step_load.wait()
    for copy in gate_loads:
        copy.wait()
    for offset in range(n_z):
        across(offset).wait_recv()

    which = step_now[0]
    gate_row = gates[0, pl.ds(which, 1), :]
    slope_row = gates[1, pl.ds(which, 1), :]
    span = n_z * shard
    for height in range(n_h):
        outs = slice(height * span, (height + 1) * span)
        both = None
        for part in range(2):
            weight = jnp.concatenate(
                [wbuf[part, i, height * shard : (height + 1) * shard, :] for i in range(n_z)], 0
            )
            term = lax.dot_general(
                attn[:, part * khalf : (part + 1) * khalf],
                weight,
                NT,
                preferred_element_type=jnp.float32,
            )
            both = term if both is None else both + term
        gate = gate_row[:, outs]
        outp_ref[:, outs] = (gate * both[:tokens]).astype(outp_ref.dtype)
        tangent = gate * both[tokens:] + slope_row[:, outs] * both[:tokens]
        outt_ref[:, outs] = tangent.astype(outt_ref.dtype)

    def finish(g, carry):
        to_partner(g).wait_send()

        @pl.when(has_left)
        def _():
            own_left(g).wait_send()
            relay_left(g).wait_send()

        @pl.when(has_right)
        def _():
            own_right(g).wait_send()
            relay_right(g).wait_send()

        return carry

    lax.fori_loop(0, chunks, finish, 0)
    to_p.wait_send()
    to_g.wait_send()
    on_g.wait_send()
    for step in range(hops):
        for sub in range(2):
            if step < hops - 1 or sub == 0:
                ring_up(step, sub).wait_send()
            if step < hops - 1 or sub == 1:
                ring_down(step, sub).wait_send()
    for offset in range(n_z):
        across(offset).wait_send()


def local(sizes, q, k, v, qt, kt, vt, weight, gate_table, gate_slope, timestep):
    _, frames, rows, cols, features = q.shape
    tokens = frames * rows * cols
    frame = rows * cols
    shard = weight.shape[1]
    n_tm, n_h, n_z = sizes
    chunks = features // (PAIR * HD)
    flat = [a.reshape(tokens, features) for a in (q, k, v, qt, kt, vt)]
    steps = gate_table.shape[0]
    dma = pltpu.SemaphoreType.DMA
    dims = (n_tm, n_h, n_z, tokens, frame, features, shard)
    weights = 3 + 2 * n_z + n_z
    anywhere = pl.BlockSpec(memory_space=pl.ANY)
    out = jax.ShapeDtypeStruct((tokens, features), jnp.bfloat16)
    out_p, out_t = pl.pallas_call(
        functools.partial(kernel, dims),
        out_shape=(out, out),
        in_specs=[pl.BlockSpec(memory_space=pltpu.HBM)] + [anywhere] * 9,
        out_specs=(pl.BlockSpec(memory_space=pltpu.VMEM),) * 2,
        scratch_shapes=[
            pltpu.VMEM((4, 2 * tokens + 4 * frame, features), jnp.bfloat16),
            pltpu.VMEM((2, tokens, features), jnp.bfloat16),
            pltpu.VMEM((2 * tokens, features), jnp.bfloat16),
            pltpu.VMEM((2, n_z, n_h * shard, features // 2), jnp.bfloat16),
            pltpu.VMEM((2, steps, features), jnp.float32),
            pltpu.SMEM((1,), jnp.int32),
            pltpu.SemaphoreType.REGULAR((2,)),
            dma((10,)),
        ]
        + [dma((chunks,))] * 10
        + [dma((weights,))] * 2,
        compiler_params=pltpu.CompilerParams(collective_id=0, has_side_effects=True),
        name="tiled_attention",
    )(timestep, *flat, weight.T, gate_table, gate_slope)
    return (out_p.reshape(q.shape), out_t.reshape(q.shape))


def solution(mesh):
    spec = P("fsdp", "tm", "height", None, None)
    in_specs = (spec,) * 6 + (P(None, ("height", "fsdp")), P(None, None), P(None, None), P("fsdp"))
    sizes = (mesh.shape["tm"], mesh.shape["height"], mesh.shape["fsdp"])
    return jax.shard_map(
        functools.partial(local, sizes),
        mesh=mesh,
        in_specs=in_specs,
        out_specs=(spec, spec),
        check_vma=False,
    )
```

```python
import functools
import math

import jax
import jax.numpy as jnp
from jax import lax
from jax.experimental import pallas as pl
from jax.experimental.pallas import tpu as pltpu
from jax.sharding import PartitionSpec as P

HD = 128
PAIR = 2
MESH = pl.DeviceIdType.MESH
NT = (((1,), (1,)), ((), ()))


def kernel(
    dims,
    step_ref,
    q_ref,
    k_ref,
    v_ref,
    qt_ref,
    kt_ref,
    vt_ref,
    w_ref,
    gate_ref,
    slope_ref,
    outp_ref,
    outt_ref,
    kv,
    qq,
    attn,
    wbuf,
    gates,
    step_now,
    hello,
    load_sem,
    part_s,
    part_r,
    ownl_s,
    ownl_r,
    ownr_s,
    ownr_r,
    rell_s,
    rell_r,
    relr_s,
    relr_r,
    ws,
    wr,
):
    n_tm, n_h, n_z, tokens, frame, features, shard = dims
    chunks = features // (PAIR * HD)
    wide = PAIR * HD
    khalf = features // 2
    half_tm = n_tm // 2
    tm = lax.axis_index("tm")
    h = lax.axis_index("height")
    z = lax.axis_index("fsdp")
    core = lax.rem(tm, 2)
    twin = h + 1 - 2 * lax.rem(h, 2)
    partner = (tm, twin, z)
    outer = jnp.logical_or(h == 0, h == n_h - 1)
    gap = (jnp.where(outer, lax.rem(tm + half_tm, n_tm), tm), n_h - 1 - h, z)
    z_up = lax.rem(z + 1, n_z)
    z_down = lax.rem(z + n_z - 1, n_z)
    above = (tm, h, z_up)
    below = (tm, h, z_down)
    left = (tm - 1, h, z)
    right = (tm + 1, h, z)
    sibling = (tm + 1 - 2 * core, h, z)
    has_left = tm > 0
    has_right = tm < n_tm - 1
    cross_left = tm == half_tm
    cross_right = tm == half_tm - 1

    own = 0
    other = tokens
    left_own = 2 * tokens
    left_other = left_own + frame
    right_own = left_other + frame
    right_other = right_own + frame
    last = tokens - frame

    even = lax.rem(tm + h + z, 2) == 0
    odd = jnp.logical_not(even)
    barrier = pltpu.get_barrier_semaphore()
    always = tm >= 0
    others = (
        (gap, always, 1, 1),
        (left, has_left, 3, 2),
        (right, has_right, 2, 3),
        (above, always, 5, 4),
        (below, always, 4, 5),
    )

    def signal(semaphore, peer):
        pl.semaphore_signal(semaphore, inc=1, device_id=peer, device_id_type=MESH)

    @pl.when(even)
    def _():
        signal(barrier, partner)

    @pl.when(odd)
    def _():
        for peer, exists, _, _ in others:

            @pl.when(exists)
            def _():
                signal(barrier, peer)

    kv_loads = [
        pltpu.make_async_copy(ref, kv.at[i, pl.ds(own, tokens)], load_sem.at[i])
        for i, ref in enumerate((k_ref, v_ref, kt_ref, vt_ref))
    ]
    q_loads = [
        pltpu.make_async_copy(ref, qq.at[i], load_sem.at[4 + i])
        for i, ref in enumerate((q_ref, qt_ref))
    ]
    gate_loads = [
        pltpu.make_async_copy(ref, gates.at[i], load_sem.at[6 + i])
        for i, ref in enumerate((gate_ref, slope_ref))
    ]
    columns = pl.ds(pl.multiple_of(core * khalf, HD), khalf)

    def shard_of(height):
        return wbuf.at[core, z, pl.ds(pl.multiple_of(height * shard, 16), shard)]

    w_load = pltpu.make_async_copy(w_ref.at[:, columns], shard_of(h), load_sem.at[8])
    step_load = pltpu.make_async_copy(step_ref, step_now, load_sem.at[9])
    w_load.start()
    for copy in kv_loads + q_loads + gate_loads + [step_load]:
        copy.start()

    rows = 2 * frame

    @pl.when(jnp.logical_not(has_left))
    def _():
        kv[:, pl.ds(left_own, rows), :] = jnp.zeros((4, rows, features), kv.dtype)

    @pl.when(jnp.logical_not(has_right))
    def _():
        kv[:, pl.ds(right_own, rows), :] = jnp.zeros((4, rows, features), kv.dtype)

    @pl.when(odd)
    def _():
        pl.semaphore_wait(barrier, 1)
        signal(hello.at[0], partner)

    @pl.when(even)
    def _():
        pl.semaphore_wait(hello.at[0], 1)

    w_load.wait()
    for copy in kv_loads:
        copy.wait()

    def move(source, target, send, recv, device):
        return pltpu.make_async_remote_copy(
            src_ref=source,
            dst_ref=target,
            send_sem=send,
            recv_sem=recv,
            device_id=device,
            device_id_type=MESH,
        )

    def block(row, count, g):
        cols = pl.ds(pl.multiple_of(g * wide, wide), wide)
        return kv.at[:, pl.ds(row, count), cols]

    pieces = ((0, frame), (last, frame), (frame, tokens - 2 * frame))

    def to_partner(g, piece):
        row, count = pieces[piece]
        slot = g * 3 + piece
        return move(block(own + row, count, g), block(other + row, count, g), part_s.at[slot], part_r.at[slot], partner)

    def send_edges(g):
        to_partner(g, 0).start()
        to_partner(g, 1).start()

    def send_middle(g):
        to_partner(g, 2).start()

    def own_left(g):
        return move(block(own, frame, g), block(right_own, frame, g), ownl_s.at[g], ownr_r.at[g], left)

    def own_right(g):
        return move(block(last, frame, g), block(left_own, frame, g), ownr_s.at[g], ownl_r.at[g], right)

    def relay_left(g):
        return move(block(other, frame, g), block(right_other, frame, g), rell_s.at[g], relr_r.at[g], left)

    def relay_right(g):
        return move(block(other + last, frame, g), block(left_other, frame, g), relr_s.at[g], rell_r.at[g], right)

    def cross_to_left(g):
        return move(block(left_own, frame, g), block(left_other, frame, g), rell_s.at[g], rell_r.at[g], partner)

    def cross_to_right(g):
        return move(block(right_own, frame, g), block(right_other, frame, g), relr_s.at[g], relr_r.at[g], partner)

    def shard_move(height, slot, device):
        return move(shard_of(height), shard_of(height), ws.at[slot], wr.at[slot], device)

    to_p = shard_move(h, 0, partner)
    to_g = shard_move(h, 1, gap)
    on_g = shard_move(twin, 2, gap)

    hops = n_z // 2
    half_rows = n_h * shard // 2

    pair_row = pl.multiple_of(lax.div(h, 2) * half_rows, 16)
    far_row = pl.multiple_of(half_rows - lax.div(h, 2) * half_rows, 16)

    def z_block(which, sub):
        return wbuf.at[core, which, pl.ds(far_row if sub else pair_row, half_rows)]

    def ring_up(step, sub):
        ref = z_block(lax.rem(z + n_z - step, n_z), sub)
        slot = 3 + 2 * step + sub
        return move(ref, ref, ws.at[slot], wr.at[slot], above)

    def ring_down(step, sub):
        ref = z_block(lax.rem(z + step, n_z), sub)
        slot = 3 + 2 * hops + 2 * step + sub
        return move(ref, ref, ws.at[slot], wr.at[slot], below)

    def across(offset):
        ref = wbuf.at[core, lax.rem(z + offset, n_z)]
        slot = 3 + 4 * hops + offset
        return move(ref, ref, ws.at[slot], wr.at[slot], sibling)

    crosses = jnp.logical_or(cross_left, cross_right)
    to_p.start()

    def send_chunks(first, stop):
        for k in range(first, stop):
            if k == 0:
                send_edges(0)
            if k + 1 < chunks:
                send_edges(k + 1)
            send_middle(k)

    send_chunks(0, 2)

    @pl.when(jnp.logical_not(crosses))
    def _():
        send_chunks(2, chunks)

    @pl.when(even)
    def _():
        count = 3 + has_left.astype(jnp.int32) + has_right.astype(jnp.int32)
        pl.semaphore_wait(barrier, count)
        for peer, exists, slot, _ in others:

            @pl.when(exists)
            def _():
                signal(hello.at[slot], peer)

    @pl.when(odd)
    def _():
        for _, exists, _, slot in others:

            @pl.when(exists)
            def _():
                pl.semaphore_wait(hello.at[slot], 1)

    to_g.start()

    def send_own(g, carry):
        @pl.when(jnp.logical_and(has_left, jnp.logical_or(g < 2, jnp.logical_not(cross_left))))
        def _():
            own_left(g).start()

        @pl.when(jnp.logical_and(has_right, jnp.logical_or(g < 2, jnp.logical_not(cross_right))))
        def _():
            own_right(g).start()

        return carry

    lax.fori_loop(0, chunks, send_own, 0)

    to_p.wait_recv()
    on_g.start()
    ring_up(0, 0).start()
    ring_down(0, 0).start()

    for copy in q_loads:
        copy.wait()

    scaling = 1.0 / math.sqrt(HD)
    spot = lax.broadcasted_iota(jnp.int32, (1, 4 * frame), 1)
    hidden = jnp.logical_or(
        jnp.logical_and(jnp.logical_not(has_left), spot < 2 * frame),
        jnp.logical_and(jnp.logical_not(has_right), spot >= 2 * frame),
    )
    bias = jnp.where(hidden, -1e30, 0.0).astype(jnp.float32)

    def attend(cols):
        q, qt = qq[0, :, cols], qq[1, :, cols]
        k, v, kt, vt = (kv[i, :, cols] for i in range(4))
        scores = lax.dot_general(q, k, NT, preferred_element_type=jnp.float32) * scaling
        scores = jnp.concatenate([scores[:, : 2 * tokens], scores[:, 2 * tokens :] + bias], 1)
        lifted = jnp.exp(scores - jnp.max(scores, axis=-1, keepdims=True))
        probs = lifted * (1.0 / jnp.sum(lifted, axis=-1, keepdims=True))
        low = probs.astype(jnp.bfloat16)
        slopes = (
            lax.dot_general(
                jnp.concatenate([qt, q], 1),
                jnp.concatenate([k, kt], 1),
                NT,
                preferred_element_type=jnp.float32,
            )
            * scaling
        )
        centre = jnp.sum(probs * slopes, axis=-1, keepdims=True)
        bent = (probs * (slopes - centre)).astype(jnp.bfloat16)
        primal = jnp.dot(low, v, preferred_element_type=jnp.float32)
        tangent = jnp.dot(bent, v, preferred_element_type=jnp.float32)
        tangent = tangent + jnp.dot(low, vt, preferred_element_type=jnp.float32)
        attn[pl.ds(0, tokens), cols] = primal.astype(jnp.bfloat16)
        attn[pl.ds(tokens, tokens), cols] = tangent.astype(jnp.bfloat16)

    def ring_pass(step, sub):
        ups = step < hops or sub == 0
        downs = step < hops or sub == 1
        if ups:
            ring_up(step - 1, sub).wait_recv()
        if downs:
            ring_down(step - 1, sub).wait_recv()
        if step < hops - 1 or (step == hops - 1 and sub == 0):
            ring_up(step, sub).start()
        if step < hops - 1 or (step == hops - 1 and sub == 1):
            ring_down(step, sub).start()

    def ring_stage(g):
        if g == 0:
            to_g.wait_recv()
            on_g.wait_recv()
            ring_up(0, 1).start()
            ring_down(0, 1).start()
            across(0).start()
        if 1 <= g <= hops:
            ring_pass(g, 1)
            if g < hops:
                across(n_z - g).start()
                across(g).start()
            else:
                across(hops).start()
        if g < hops:
            ring_pass(g + 1, 0)

    def forward(g):
        for k in range(2):

            @pl.when(jnp.logical_and(cross_left, g < chunks // 2 - 1))
            def _():
                own_left(2 * g + 2 + k).start()

            @pl.when(jnp.logical_and(cross_right, g < chunks // 2 - 1))
            def _():
                own_right(2 * g + 2 + k).start()

        to_partner(g, 0).wait_recv()
        to_partner(g, 1).wait_recv()

        @pl.when(jnp.logical_and(has_left, jnp.logical_not(cross_left)))
        def _():
            relay_left(g).start()

        @pl.when(jnp.logical_and(has_right, jnp.logical_not(cross_right)))
        def _():
            relay_right(g).start()

        @pl.when(cross_left)
        def _():
            own_right(g).wait_recv()
            cross_to_left(g).start()

        @pl.when(cross_right)
        def _():
            own_left(g).wait_recv()
            cross_to_right(g).start()

        @pl.when(jnp.logical_and(crosses, g < chunks - 2))
        def _():
            @pl.when(g < chunks - 3)
            def _():
                send_edges(g + 3)

            send_middle(g + 2)

    def compute(g):
        to_partner(g, 2).wait_recv()

        @pl.when(jnp.logical_and(has_left, jnp.logical_not(cross_left)))
        def _():
            own_right(g).wait_recv()

        @pl.when(jnp.logical_and(has_right, jnp.logical_not(cross_right)))
        def _():
            own_left(g).wait_recv()

        @pl.when(has_left)
        def _():
            relay_right(g).wait_recv()

        @pl.when(has_right)
        def _():
            relay_left(g).wait_recv()

        for head in range(PAIR):
            attend(pl.ds(pl.multiple_of(g * wide + head * HD, HD), HD))

    lag = jnp.where(crosses, 2, 1)
    shift = jnp.where(z < 2, 2, jnp.where(z < n_z // 2, 1, 0))

    def chunk(g, carry):
        @pl.when(g < chunks)
        def _():
            forward(g)

        for stage in range(hops + 1):

            @pl.when(g == stage + shift)
            def _():
                ring_stage(stage)

        @pl.when(jnp.logical_and(g >= lag, g < chunks + lag))
        def _():
            compute(g - lag)

        return carry

    lax.fori_loop(0, chunks + 2, chunk, 0)

    step_load.wait()
    for copy in gate_loads:
        copy.wait()
    for offset in range(n_z):
        across(offset).wait_recv()

    which = step_now[0]
    gate_row = gates[0, pl.ds(which, 1), :]
    slope_row = gates[1, pl.ds(which, 1), :]
    span = n_z * shard
    for height in range(n_h):
        outs = slice(height * span, (height + 1) * span)
        both = None
        for part in range(2):
            weight = jnp.concatenate(
                [wbuf[part, i, height * shard : (height + 1) * shard, :] for i in range(n_z)], 0
            )
            term = lax.dot_general(
                attn[:, part * khalf : (part + 1) * khalf],
                weight,
                NT,
                preferred_element_type=jnp.float32,
            )
            both = term if both is None else both + term
        gate = gate_row[:, outs]
        outp_ref[:, outs] = (gate * both[:tokens]).astype(outp_ref.dtype)
        tangent = gate * both[tokens:] + slope_row[:, outs] * both[:tokens]
        outt_ref[:, outs] = tangent.astype(outt_ref.dtype)

    def finish(g, carry):
        for piece in range(3):
            to_partner(g, piece).wait_send()

        @pl.when(has_left)
        def _():
            own_left(g).wait_send()
            relay_left(g).wait_send()

        @pl.when(has_right)
        def _():
            own_right(g).wait_send()
            relay_right(g).wait_send()

        return carry

    lax.fori_loop(0, chunks, finish, 0)
    to_p.wait_send()
    to_g.wait_send()
    on_g.wait_send()
    for step in range(hops):
        for sub in range(2):
            if step < hops - 1 or sub == 0:
                ring_up(step, sub).wait_send()
            if step < hops - 1 or sub == 1:
                ring_down(step, sub).wait_send()
    for offset in range(n_z):
        across(offset).wait_send()


def local(sizes, q, k, v, qt, kt, vt, weight, gate_table, gate_slope, timestep):
    _, frames, rows, cols, features = q.shape
    tokens = frames * rows * cols
    frame = rows * cols
    shard = weight.shape[1]
    n_tm, n_h, n_z = sizes
    chunks = features // (PAIR * HD)
    flat = [pltpu.with_memory_space_constraint(a.reshape(tokens, features), pltpu.HBM) for a in (q, k, v, qt, kt, vt)]
    steps = gate_table.shape[0]
    dma = pltpu.SemaphoreType.DMA
    dims = (n_tm, n_h, n_z, tokens, frame, features, shard)
    weights = 3 + 2 * n_z + n_z
    anywhere = pl.BlockSpec(memory_space=pl.ANY)
    out = jax.ShapeDtypeStruct((tokens, features), jnp.bfloat16)
    out_p, out_t = pl.pallas_call(
        functools.partial(kernel, dims),
        out_shape=(out, out),
        in_specs=[pl.BlockSpec(memory_space=pltpu.HBM)] + [anywhere] * 9,
        out_specs=(pl.BlockSpec(memory_space=pltpu.VMEM),) * 2,
        scratch_shapes=[
            pltpu.VMEM((4, 2 * tokens + 4 * frame, features), jnp.bfloat16),
            pltpu.VMEM((2, tokens, features), jnp.bfloat16),
            pltpu.VMEM((2 * tokens, features), jnp.bfloat16),
            pltpu.VMEM((2, n_z, n_h * shard, features // 2), jnp.bfloat16),
            pltpu.VMEM((2, steps, features), jnp.float32),
            pltpu.SMEM((1,), jnp.int32),
            pltpu.SemaphoreType.REGULAR((6,)),
            dma((10,)),
        ]
        + [dma((3 * chunks,))] * 2
        + [dma((chunks,))] * 8
        + [dma((weights,))] * 2,
        compiler_params=pltpu.CompilerParams(vmem_limit_bytes=24 << 20, collective_id=0, has_side_effects=True),
        name="tiled_attention",
    )(timestep, *flat, *(pltpu.with_memory_space_constraint(a, pltpu.HBM) for a in (weight.T, gate_table, gate_slope)))
    return (out_p.reshape(q.shape), out_t.reshape(q.shape))


def solution(mesh):
    spec = P("fsdp", "tm", "height", None, None)
    in_specs = (spec,) * 6 + (P(None, ("height", "fsdp")), P(None, None), P(None, None), P("fsdp"))
    sizes = (mesh.shape["tm"], mesh.shape["height"], mesh.shape["fsdp"])
    return jax.shard_map(
        functools.partial(local, sizes),
        mesh=mesh,
        in_specs=in_specs,
        out_specs=(spec, spec),
        check_vma=False,
    )
```

```python
import functools
import math

import jax
import jax.numpy as jnp
from jax import lax
from jax.experimental import pallas as pl
from jax.experimental.pallas import tpu as pltpu
from jax.sharding import PartitionSpec as P

HD = 128
PAIR = 2
MESH = pl.DeviceIdType.MESH
NT = (((1,), (1,)), ((), ()))


def kernel(
    dims,
    step_ref,
    q_ref,
    k_ref,
    v_ref,
    qt_ref,
    kt_ref,
    vt_ref,
    w_ref,
    gate_ref,
    slope_ref,
    outp_ref,
    outt_ref,
    kv,
    qq,
    attn,
    wbuf,
    gates,
    step_now,
    hello,
    load_sem,
    part_s,
    part_r,
    ownl_s,
    ownl_r,
    ownr_s,
    ownr_r,
    rell_s,
    rell_r,
    relr_s,
    relr_r,
    ws,
    wr,
):
    n_tm, n_h, n_z, tokens, frame, features, shard = dims
    chunks = features // (PAIR * HD)
    wide = PAIR * HD
    khalf = features // 2
    half_tm = n_tm // 2
    tm = lax.axis_index("tm")
    h = lax.axis_index("height")
    z = lax.axis_index("fsdp")
    core = lax.rem(tm, 2)
    twin = h + 1 - 2 * lax.rem(h, 2)
    partner = (tm, twin, z)
    outer = jnp.logical_or(h == 0, h == n_h - 1)
    gap = (jnp.where(outer, lax.rem(tm + half_tm, n_tm), tm), n_h - 1 - h, z)
    z_up = lax.rem(z + 1, n_z)
    z_down = lax.rem(z + n_z - 1, n_z)
    above = (tm, h, z_up)
    below = (tm, h, z_down)
    left = (tm - 1, h, z)
    right = (tm + 1, h, z)
    sibling = (tm + 1 - 2 * core, h, z)
    has_left = tm > 0
    has_right = tm < n_tm - 1
    cross_left = tm == half_tm
    cross_right = tm == half_tm - 1

    own = 0
    other = tokens
    left_own = 2 * tokens
    left_other = left_own + frame
    right_own = left_other + frame
    right_other = right_own + frame
    last = tokens - frame

    even = lax.rem(tm + h + z, 2) == 0
    odd = jnp.logical_not(even)
    barrier = pltpu.get_barrier_semaphore()
    always = tm >= 0
    others = (
        (gap, always, 1, 1),
        (left, has_left, 3, 2),
        (right, has_right, 2, 3),
        (above, always, 5, 4),
        (below, always, 4, 5),
    )

    def signal(semaphore, peer):
        pl.semaphore_signal(semaphore, inc=1, device_id=peer, device_id_type=MESH)

    @pl.when(even)
    def _():
        signal(barrier, partner)

    @pl.when(odd)
    def _():
        for peer, exists, _, _ in others:

            @pl.when(exists)
            def _():
                signal(barrier, peer)

    kv_loads = [
        pltpu.make_async_copy(ref, kv.at[i, pl.ds(own, tokens)], load_sem.at[i])
        for i, ref in enumerate((k_ref, v_ref, kt_ref, vt_ref))
    ]
    q_loads = [
        pltpu.make_async_copy(ref, qq.at[i], load_sem.at[4 + i])
        for i, ref in enumerate((q_ref, qt_ref))
    ]
    gate_loads = [
        pltpu.make_async_copy(ref, gates.at[i], load_sem.at[6 + i])
        for i, ref in enumerate((gate_ref, slope_ref))
    ]
    columns = pl.ds(pl.multiple_of(core * khalf, HD), khalf)

    def shard_of(height):
        return wbuf.at[core, z, pl.ds(pl.multiple_of(height * shard, 16), shard)]

    w_load = pltpu.make_async_copy(w_ref.at[:, columns], shard_of(h), load_sem.at[8])
    step_load = pltpu.make_async_copy(step_ref, step_now, load_sem.at[9])
    w_load.start()
    for copy in kv_loads + q_loads + gate_loads + [step_load]:
        copy.start()

    rows = 2 * frame

    @pl.when(jnp.logical_not(has_left))
    def _():
        kv[:, pl.ds(left_own, rows), :] = jnp.zeros((4, rows, features), kv.dtype)

    @pl.when(jnp.logical_not(has_right))
    def _():
        kv[:, pl.ds(right_own, rows), :] = jnp.zeros((4, rows, features), kv.dtype)

    @pl.when(odd)
    def _():
        pl.semaphore_wait(barrier, 1)
        signal(hello.at[0], partner)

    @pl.when(even)
    def _():
        pl.semaphore_wait(hello.at[0], 1)

    w_load.wait()
    for copy in kv_loads:
        copy.wait()

    def move(source, target, send, recv, device):
        return pltpu.make_async_remote_copy(
            src_ref=source,
            dst_ref=target,
            send_sem=send,
            recv_sem=recv,
            device_id=device,
            device_id_type=MESH,
        )

    def block(row, count, g):
        cols = pl.ds(pl.multiple_of(g * wide, wide), wide)
        return kv.at[:, pl.ds(row, count), cols]

    pieces = ((0, frame), (last, frame), (frame, tokens - 2 * frame))

    def to_partner(g, piece):
        row, count = pieces[piece]
        slot = g * 3 + piece
        return move(block(own + row, count, g), block(other + row, count, g), part_s.at[slot], part_r.at[slot], partner)

    def send_edges(g):
        to_partner(g, 0).start()
        to_partner(g, 1).start()

    def send_middle(g):
        to_partner(g, 2).start()

    def own_left(g):
        return move(block(own, frame, g), block(right_own, frame, g), ownl_s.at[g], ownr_r.at[g], left)

    def own_right(g):
        return move(block(last, frame, g), block(left_own, frame, g), ownr_s.at[g], ownl_r.at[g], right)

    def relay_left(g):
        return move(block(other, frame, g), block(right_other, frame, g), rell_s.at[g], relr_r.at[g], left)

    def relay_right(g):
        return move(block(other + last, frame, g), block(left_other, frame, g), relr_s.at[g], rell_r.at[g], right)

    def cross_to_left(g):
        return move(block(left_own, frame, g), block(left_other, frame, g), rell_s.at[g], rell_r.at[g], partner)

    def cross_to_right(g):
        return move(block(right_own, frame, g), block(right_other, frame, g), relr_s.at[g], relr_r.at[g], partner)

    def shard_move(height, slot, device):
        return move(shard_of(height), shard_of(height), ws.at[slot], wr.at[slot], device)

    to_p = shard_move(h, 0, partner)
    to_g = shard_move(h, 1, gap)
    on_g = shard_move(twin, 2, gap)

    hops = n_z // 2
    half_rows = n_h * shard // 2

    pair_row = pl.multiple_of(lax.div(h, 2) * half_rows, 16)
    far_row = pl.multiple_of(half_rows - lax.div(h, 2) * half_rows, 16)

    def z_block(which, sub):
        return wbuf.at[core, which, pl.ds(far_row if sub else pair_row, half_rows)]

    def ring_up(step, sub):
        ref = z_block(lax.rem(z + n_z - step, n_z), sub)
        slot = 3 + 2 * step + sub
        return move(ref, ref, ws.at[slot], wr.at[slot], above)

    def ring_down(step, sub):
        ref = z_block(lax.rem(z + step, n_z), sub)
        slot = 3 + 2 * hops + 2 * step + sub
        return move(ref, ref, ws.at[slot], wr.at[slot], below)

    def across(offset):
        ref = wbuf.at[core, lax.rem(z + offset, n_z)]
        slot = 3 + 4 * hops + offset
        return move(ref, ref, ws.at[slot], wr.at[slot], sibling)

    crosses = jnp.logical_or(cross_left, cross_right)
    to_p.start()

    def send_chunks(first, stop):
        for k in range(first, stop):
            if k == 0:
                send_edges(0)
            if k + 1 < chunks:
                send_edges(k + 1)
            send_middle(k)

    send_chunks(0, 2)

    @pl.when(jnp.logical_not(crosses))
    def _():
        send_chunks(2, chunks)

    @pl.when(even)
    def _():
        count = 3 + has_left.astype(jnp.int32) + has_right.astype(jnp.int32)
        pl.semaphore_wait(barrier, count)
        for peer, exists, slot, _ in others:

            @pl.when(exists)
            def _():
                signal(hello.at[slot], peer)

    @pl.when(odd)
    def _():
        for _, exists, _, slot in others:

            @pl.when(exists)
            def _():
                pl.semaphore_wait(hello.at[slot], 1)

    to_g.start()

    def send_own(g, carry):
        @pl.when(jnp.logical_and(has_left, jnp.logical_not(cross_left)))
        def _():
            own_left(g).start()

        @pl.when(jnp.logical_and(has_right, jnp.logical_not(cross_right)))
        def _():
            own_right(g).start()

        return carry

    lax.fori_loop(0, chunks, send_own, 0)

    to_p.wait_recv()
    on_g.start()
    ring_up(0, 0).start()
    ring_down(0, 0).start()

    for copy in q_loads:
        copy.wait()

    scaling = 1.0 / math.sqrt(HD)
    spot = lax.broadcasted_iota(jnp.int32, (1, 4 * frame), 1)
    hidden = jnp.logical_or(
        jnp.logical_and(jnp.logical_not(has_left), spot < 2 * frame),
        jnp.logical_and(jnp.logical_not(has_right), spot >= 2 * frame),
    )
    bias = jnp.where(hidden, -1e30, 0.0).astype(jnp.float32)

    def attend(cols):
        q, qt = qq[0, :, cols], qq[1, :, cols]
        k, v, kt, vt = (kv[i, :, cols] for i in range(4))
        scores = lax.dot_general(q, k, NT, preferred_element_type=jnp.float32) * scaling
        scores = jnp.concatenate([scores[:, : 2 * tokens], scores[:, 2 * tokens :] + bias], 1)
        lifted = jnp.exp(scores - jnp.max(scores, axis=-1, keepdims=True))
        probs = lifted * (1.0 / jnp.sum(lifted, axis=-1, keepdims=True))
        low = probs.astype(jnp.bfloat16)
        slopes = (
            lax.dot_general(
                jnp.concatenate([qt, q], 1),
                jnp.concatenate([k, kt], 1),
                NT,
                preferred_element_type=jnp.float32,
            )
            * scaling
        )
        centre = jnp.sum(probs * slopes, axis=-1, keepdims=True)
        bent = (probs * (slopes - centre)).astype(jnp.bfloat16)
        primal = jnp.dot(low, v, preferred_element_type=jnp.float32)
        tangent = jnp.dot(bent, v, preferred_element_type=jnp.float32)
        tangent = tangent + jnp.dot(low, vt, preferred_element_type=jnp.float32)
        attn[pl.ds(0, tokens), cols] = primal.astype(jnp.bfloat16)
        attn[pl.ds(tokens, tokens), cols] = tangent.astype(jnp.bfloat16)

    def ring_pass(step, sub):
        ups = step < hops or sub == 0
        downs = step < hops or sub == 1
        if ups:
            ring_up(step - 1, sub).wait_recv()
        if downs:
            ring_down(step - 1, sub).wait_recv()
        if step < hops - 1 or (step == hops - 1 and sub == 0):
            ring_up(step, sub).start()
        if step < hops - 1 or (step == hops - 1 and sub == 1):
            ring_down(step, sub).start()

    def ring_stage(g):
        if g == 0:
            to_g.wait_recv()
            on_g.wait_recv()
            ring_up(0, 1).start()
            ring_down(0, 1).start()
            across(0).start()
        if 1 <= g <= hops:
            ring_pass(g, 1)
            if g < hops:
                across(n_z - g).start()
                across(g).start()
            else:
                across(hops).start()
        if g < hops:
            ring_pass(g + 1, 0)

    def forward(g):
        @pl.when(jnp.logical_and(cross_left, g == 0))
        def _():
            own_left(0).start()

        @pl.when(jnp.logical_and(cross_right, g == 0))
        def _():
            own_right(0).start()

        @pl.when(jnp.logical_and(cross_left, g < chunks - 1))
        def _():
            own_left(g + 1).start()

        @pl.when(jnp.logical_and(cross_right, g < chunks - 1))
        def _():
            own_right(g + 1).start()

        to_partner(g, 0).wait_recv()
        to_partner(g, 1).wait_recv()

        @pl.when(jnp.logical_and(has_left, jnp.logical_not(cross_left)))
        def _():
            relay_left(g).start()

        @pl.when(jnp.logical_and(has_right, jnp.logical_not(cross_right)))
        def _():
            relay_right(g).start()

        @pl.when(cross_left)
        def _():
            own_right(g).wait_recv()
            cross_to_left(g).start()

        @pl.when(cross_right)
        def _():
            own_left(g).wait_recv()
            cross_to_right(g).start()

        @pl.when(jnp.logical_and(crosses, g < chunks - 2))
        def _():
            @pl.when(g < chunks - 3)
            def _():
                send_edges(g + 3)

            send_middle(g + 2)

    def compute(g):
        to_partner(g, 2).wait_recv()

        @pl.when(jnp.logical_and(has_left, jnp.logical_not(cross_left)))
        def _():
            own_right(g).wait_recv()

        @pl.when(jnp.logical_and(has_right, jnp.logical_not(cross_right)))
        def _():
            own_left(g).wait_recv()

        @pl.when(has_left)
        def _():
            relay_right(g).wait_recv()

        @pl.when(has_right)
        def _():
            relay_left(g).wait_recv()

        for head in range(PAIR):
            attend(pl.ds(pl.multiple_of(g * wide + head * HD, HD), HD))

    lag = jnp.where(crosses, 2, 1)
    shift = jnp.where(z < 2, 2, jnp.where(z < n_z // 2, 1, 0))

    def chunk(g, carry):
        @pl.when(g < chunks)
        def _():
            forward(g)

        for stage in range(hops + 1):

            @pl.when(g == stage + shift)
            def _():
                ring_stage(stage)

        @pl.when(jnp.logical_and(g >= lag, g < chunks + lag))
        def _():
            compute(g - lag)

        return carry

    lax.fori_loop(0, chunks + 2, chunk, 0)

    step_load.wait()
    for copy in gate_loads:
        copy.wait()
    for offset in range(n_z):
        across(offset).wait_recv()

    which = step_now[0]
    gate_row = gates[0, pl.ds(which, 1), :]
    slope_row = gates[1, pl.ds(which, 1), :]
    span = n_z * shard
    for height in range(n_h):
        outs = slice(height * span, (height + 1) * span)
        both = None
        for part in range(2):
            weight = jnp.concatenate(
                [wbuf[part, i, height * shard : (height + 1) * shard, :] for i in range(n_z)], 0
            )
            term = lax.dot_general(
                attn[:, part * khalf : (part + 1) * khalf],
                weight,
                NT,
                preferred_element_type=jnp.float32,
            )
            both = term if both is None else both + term
        gate = gate_row[:, outs]
        outp_ref[:, outs] = (gate * both[:tokens]).astype(outp_ref.dtype)
        tangent = gate * both[tokens:] + slope_row[:, outs] * both[:tokens]
        outt_ref[:, outs] = tangent.astype(outt_ref.dtype)

    def finish(g, carry):
        for piece in range(3):
            to_partner(g, piece).wait_send()

        @pl.when(has_left)
        def _():
            own_left(g).wait_send()
            relay_left(g).wait_send()

        @pl.when(has_right)
        def _():
            own_right(g).wait_send()
            relay_right(g).wait_send()

        return carry

    lax.fori_loop(0, chunks, finish, 0)
    to_p.wait_send()
    to_g.wait_send()
    on_g.wait_send()
    for step in range(hops):
        for sub in range(2):
            if step < hops - 1 or sub == 0:
                ring_up(step, sub).wait_send()
            if step < hops - 1 or sub == 1:
                ring_down(step, sub).wait_send()
    for offset in range(n_z):
        across(offset).wait_send()


def local(sizes, q, k, v, qt, kt, vt, weight, gate_table, gate_slope, timestep):
    _, frames, rows, cols, features = q.shape
    tokens = frames * rows * cols
    frame = rows * cols
    shard = weight.shape[1]
    n_tm, n_h, n_z = sizes
    chunks = features // (PAIR * HD)
    flat = [pltpu.with_memory_space_constraint(a.reshape(tokens, features), pltpu.HBM) for a in (q, k, v, qt, kt, vt)]
    steps = gate_table.shape[0]
    dma = pltpu.SemaphoreType.DMA
    dims = (n_tm, n_h, n_z, tokens, frame, features, shard)
    weights = 3 + 2 * n_z + n_z
    anywhere = pl.BlockSpec(memory_space=pl.ANY)
    out = jax.ShapeDtypeStruct((tokens, features), jnp.bfloat16)
    out_p, out_t = pl.pallas_call(
        functools.partial(kernel, dims),
        out_shape=(out, out),
        in_specs=[pl.BlockSpec(memory_space=pltpu.HBM)] + [anywhere] * 9,
        out_specs=(pl.BlockSpec(memory_space=pltpu.VMEM),) * 2,
        scratch_shapes=[
            pltpu.VMEM((4, 2 * tokens + 4 * frame, features), jnp.bfloat16),
            pltpu.VMEM((2, tokens, features), jnp.bfloat16),
            pltpu.VMEM((2 * tokens, features), jnp.bfloat16),
            pltpu.VMEM((2, n_z, n_h * shard, features // 2), jnp.bfloat16),
            pltpu.VMEM((2, steps, features), jnp.float32),
            pltpu.SMEM((1,), jnp.int32),
            pltpu.SemaphoreType.REGULAR((6,)),
            dma((10,)),
        ]
        + [dma((3 * chunks,))] * 2
        + [dma((chunks,))] * 8
        + [dma((weights,))] * 2,
        compiler_params=pltpu.CompilerParams(vmem_limit_bytes=24 << 20, collective_id=0, has_side_effects=True),
        name="tiled_attention",
    )(timestep, *flat, *(pltpu.with_memory_space_constraint(a, pltpu.HBM) for a in (weight.T, gate_table, gate_slope)))
    return (out_p.reshape(q.shape), out_t.reshape(q.shape))


def solution(mesh):
    spec = P("fsdp", "tm", "height", None, None)
    in_specs = (spec,) * 6 + (P(None, ("height", "fsdp")), P(None, None), P(None, None), P("fsdp"))
    sizes = (mesh.shape["tm"], mesh.shape["height"], mesh.shape["fsdp"])
    return jax.shard_map(
        functools.partial(local, sizes),
        mesh=mesh,
        in_specs=in_specs,
        out_specs=(spec, spec),
        check_vma=False,
    )
```

```python
import functools
import math

import jax
import jax.numpy as jnp
from jax import lax
from jax.experimental import pallas as pl
from jax.experimental.pallas import tpu as pltpu
from jax.sharding import PartitionSpec as P

HD = 128
PAIR = 2
MESH = pl.DeviceIdType.MESH
NT = (((1,), (1,)), ((), ()))


def kernel(
    dims,
    step_ref,
    q_ref,
    k_ref,
    v_ref,
    qt_ref,
    kt_ref,
    vt_ref,
    w_ref,
    gate_ref,
    slope_ref,
    outp_ref,
    outt_ref,
    kv,
    qq,
    attn,
    wbuf,
    gates,
    step_now,
    hello,
    load_sem,
    part_s,
    part_r,
    ownl_s,
    ownl_r,
    ownr_s,
    ownr_r,
    rell_s,
    rell_r,
    relr_s,
    relr_r,
    ws,
    wr,
):
    n_tm, n_h, n_z, tokens, frame, features, shard = dims
    chunks = features // (PAIR * HD)
    wide = PAIR * HD
    khalf = features // 2
    half_tm = n_tm // 2
    tm = lax.axis_index("tm")
    h = lax.axis_index("height")
    z = lax.axis_index("fsdp")
    core = lax.rem(tm, 2)
    twin = h + 1 - 2 * lax.rem(h, 2)
    partner = (tm, twin, z)
    outer = jnp.logical_or(h == 0, h == n_h - 1)
    gap = (jnp.where(outer, lax.rem(tm + half_tm, n_tm), tm), n_h - 1 - h, z)
    z_up = lax.rem(z + 1, n_z)
    z_down = lax.rem(z + n_z - 1, n_z)
    above = (tm, h, z_up)
    below = (tm, h, z_down)
    left = (tm - 1, h, z)
    right = (tm + 1, h, z)
    sibling = (tm + 1 - 2 * core, h, z)
    has_left = tm > 0
    has_right = tm < n_tm - 1
    cross_left = tm == half_tm
    cross_right = tm == half_tm - 1

    own = 0
    other = tokens
    left_own = 2 * tokens
    left_other = left_own + frame
    right_own = left_other + frame
    right_other = right_own + frame
    last = tokens - frame

    even = lax.rem(tm + h + z, 2) == 0
    odd = jnp.logical_not(even)
    barrier = pltpu.get_barrier_semaphore()
    always = tm >= 0
    others = (
        (gap, always, 1, 1),
        (left, has_left, 3, 2),
        (right, has_right, 2, 3),
        (above, always, 5, 4),
        (below, always, 4, 5),
    )

    def signal(semaphore, peer):
        pl.semaphore_signal(semaphore, inc=1, device_id=peer, device_id_type=MESH)

    @pl.when(even)
    def _():
        signal(barrier, partner)

    @pl.when(odd)
    def _():
        for peer, exists, _, _ in others:

            @pl.when(exists)
            def _():
                signal(barrier, peer)

    kv_loads = [
        pltpu.make_async_copy(ref, kv.at[i, pl.ds(own, tokens)], load_sem.at[i])
        for i, ref in enumerate((k_ref, v_ref, kt_ref, vt_ref))
    ]
    q_loads = [
        pltpu.make_async_copy(ref, qq.at[i], load_sem.at[4 + i])
        for i, ref in enumerate((q_ref, qt_ref))
    ]
    gate_loads = [
        pltpu.make_async_copy(ref, gates.at[i], load_sem.at[6 + i])
        for i, ref in enumerate((gate_ref, slope_ref))
    ]
    columns = pl.ds(pl.multiple_of(core * khalf, HD), khalf)

    def shard_of(height):
        return wbuf.at[core, z, pl.ds(pl.multiple_of(height * shard, 16), shard)]

    w_load = pltpu.make_async_copy(w_ref.at[:, columns], shard_of(h), load_sem.at[8])
    step_load = pltpu.make_async_copy(step_ref, step_now, load_sem.at[9])
    w_load.start()
    for copy in kv_loads + q_loads + gate_loads + [step_load]:
        copy.start()

    rows = 2 * frame

    @pl.when(jnp.logical_not(has_left))
    def _():
        kv[:, pl.ds(left_own, rows), :] = jnp.zeros((4, rows, features), kv.dtype)

    @pl.when(jnp.logical_not(has_right))
    def _():
        kv[:, pl.ds(right_own, rows), :] = jnp.zeros((4, rows, features), kv.dtype)

    @pl.when(odd)
    def _():
        pl.semaphore_wait(barrier, 1)
        signal(hello.at[0], partner)

    @pl.when(even)
    def _():
        pl.semaphore_wait(hello.at[0], 1)

    w_load.wait()
    for copy in kv_loads:
        copy.wait()

    def move(source, target, send, recv, device):
        return pltpu.make_async_remote_copy(
            src_ref=source,
            dst_ref=target,
            send_sem=send,
            recv_sem=recv,
            device_id=device,
            device_id_type=MESH,
        )

    def block(row, count, g):
        cols = pl.ds(pl.multiple_of(g * wide, wide), wide)
        return kv.at[:, pl.ds(row, count), cols]

    pieces = ((0, frame), (last, frame), (frame, tokens - 2 * frame))

    def to_partner(g, piece):
        row, count = pieces[piece]
        slot = g * 3 + piece
        return move(block(own + row, count, g), block(other + row, count, g), part_s.at[slot], part_r.at[slot], partner)

    def send_edges(g):
        to_partner(g, 0).start()
        to_partner(g, 1).start()

    def send_middle(g):
        to_partner(g, 2).start()

    def own_left(g):
        return move(block(own, frame, g), block(right_own, frame, g), ownl_s.at[g], ownr_r.at[g], left)

    def own_right(g):
        return move(block(last, frame, g), block(left_own, frame, g), ownr_s.at[g], ownl_r.at[g], right)

    def relay_left(g):
        return move(block(other, frame, g), block(right_other, frame, g), rell_s.at[g], relr_r.at[g], left)

    def relay_right(g):
        return move(block(other + last, frame, g), block(left_other, frame, g), relr_s.at[g], rell_r.at[g], right)

    def cross_to_left(g):
        return move(block(left_own, frame, g), block(left_other, frame, g), rell_s.at[g], rell_r.at[g], partner)

    def cross_to_right(g):
        return move(block(right_own, frame, g), block(right_other, frame, g), relr_s.at[g], relr_r.at[g], partner)

    def shard_move(height, slot, device):
        return move(shard_of(height), shard_of(height), ws.at[slot], wr.at[slot], device)

    to_p = shard_move(h, 0, partner)
    to_g = shard_move(h, 1, gap)
    on_g = shard_move(twin, 2, gap)

    hops = n_z // 2
    half_rows = n_h * shard // 2

    pair_row = pl.multiple_of(lax.div(h, 2) * half_rows, 16)
    far_row = pl.multiple_of(half_rows - lax.div(h, 2) * half_rows, 16)

    def z_block(which, sub):
        return wbuf.at[core, which, pl.ds(far_row if sub else pair_row, half_rows)]

    def ring_up(step, sub):
        ref = z_block(lax.rem(z + n_z - step, n_z), sub)
        slot = 3 + 2 * step + sub
        return move(ref, ref, ws.at[slot], wr.at[slot], above)

    def ring_down(step, sub):
        ref = z_block(lax.rem(z + step, n_z), sub)
        slot = 3 + 2 * hops + 2 * step + sub
        return move(ref, ref, ws.at[slot], wr.at[slot], below)

    def across(offset):
        ref = wbuf.at[core, lax.rem(z + offset, n_z)]
        slot = 3 + 4 * hops + offset
        return move(ref, ref, ws.at[slot], wr.at[slot], sibling)

    crosses = jnp.logical_or(cross_left, cross_right)
    to_p.start()

    def send_chunks(first, stop):
        for k in range(first, stop):
            if k == 0:
                send_edges(0)
            if k + 1 < chunks:
                send_edges(k + 1)
            send_middle(k)

    send_chunks(0, 2)

    @pl.when(jnp.logical_not(crosses))
    def _():
        send_chunks(2, chunks)

    @pl.when(even)
    def _():
        count = 3 + has_left.astype(jnp.int32) + has_right.astype(jnp.int32)
        pl.semaphore_wait(barrier, count)
        for peer, exists, slot, _ in others:

            @pl.when(exists)
            def _():
                signal(hello.at[slot], peer)

    @pl.when(odd)
    def _():
        for _, exists, _, slot in others:

            @pl.when(exists)
            def _():
                pl.semaphore_wait(hello.at[slot], 1)

    to_g.start()

    def send_own(g, carry):
        @pl.when(jnp.logical_and(has_left, jnp.logical_not(cross_left)))
        def _():
            own_left(g).start()

        @pl.when(jnp.logical_and(has_right, jnp.logical_not(cross_right)))
        def _():
            own_right(g).start()

        return carry

    lax.fori_loop(0, chunks, send_own, 0)

    to_p.wait_recv()
    on_g.start()
    ring_up(0, 0).start()
    ring_down(0, 0).start()

    for copy in q_loads:
        copy.wait()

    scaling = 1.0 / math.sqrt(HD)
    spot = lax.broadcasted_iota(jnp.int32, (1, 4 * frame), 1)
    hidden = jnp.logical_or(
        jnp.logical_and(jnp.logical_not(has_left), spot < 2 * frame),
        jnp.logical_and(jnp.logical_not(has_right), spot >= 2 * frame),
    )
    bias = jnp.where(hidden, -1e30, 0.0).astype(jnp.float32)

    def attend(cols):
        q, qt = qq[0, :, cols], qq[1, :, cols]
        k, v, kt, vt = (kv[i, :, cols] for i in range(4))
        scores = lax.dot_general(q, k, NT, preferred_element_type=jnp.float32) * scaling
        scores = jnp.concatenate([scores[:, : 2 * tokens], scores[:, 2 * tokens :] + bias], 1)
        lifted = jnp.exp(scores - jnp.max(scores, axis=-1, keepdims=True))
        probs = lifted * (1.0 / jnp.sum(lifted, axis=-1, keepdims=True))
        low = probs.astype(jnp.bfloat16)
        slopes = (
            lax.dot_general(
                jnp.concatenate([qt, q], 1),
                jnp.concatenate([k, kt], 1),
                NT,
                preferred_element_type=jnp.float32,
            )
            * scaling
        )
        centre = jnp.sum(probs * slopes, axis=-1, keepdims=True)
        bent = (probs * (slopes - centre)).astype(jnp.bfloat16)
        primal = jnp.dot(low, v, preferred_element_type=jnp.float32)
        tangent = jnp.dot(bent, v, preferred_element_type=jnp.float32)
        tangent = tangent + jnp.dot(low, vt, preferred_element_type=jnp.float32)
        attn[pl.ds(0, tokens), cols] = primal.astype(jnp.bfloat16)
        attn[pl.ds(tokens, tokens), cols] = tangent.astype(jnp.bfloat16)

    def ring_pass(step, sub):
        ups = step < hops or sub == 0
        downs = step < hops or sub == 1
        if ups:
            ring_up(step - 1, sub).wait_recv()
        if downs:
            ring_down(step - 1, sub).wait_recv()
        if step < hops - 1 or (step == hops - 1 and sub == 0):
            ring_up(step, sub).start()
        if step < hops - 1 or (step == hops - 1 and sub == 1):
            ring_down(step, sub).start()

    def ring_stage(g):
        if g == 0:
            to_g.wait_recv()
            on_g.wait_recv()
            ring_up(0, 1).start()
            ring_down(0, 1).start()
            across(0).start()
        if 1 <= g <= hops:
            ring_pass(g, 1)
            if g < hops:
                across(n_z - g).start()
                across(g).start()
            else:
                across(hops).start()
        if g < hops:
            ring_pass(g + 1, 0)

    def forward(g):
        @pl.when(jnp.logical_and(cross_left, g == 0))
        def _():
            own_left(0).start()

        @pl.when(jnp.logical_and(cross_right, g == 0))
        def _():
            own_right(0).start()

        @pl.when(jnp.logical_and(cross_left, g < chunks - 1))
        def _():
            own_left(g + 1).start()

        @pl.when(jnp.logical_and(cross_right, g < chunks - 1))
        def _():
            own_right(g + 1).start()

        to_partner(g, 0).wait_recv()
        to_partner(g, 1).wait_recv()

        @pl.when(jnp.logical_and(has_left, jnp.logical_not(cross_left)))
        def _():
            relay_left(g).start()

        @pl.when(jnp.logical_and(has_right, jnp.logical_not(cross_right)))
        def _():
            relay_right(g).start()

        @pl.when(cross_left)
        def _():
            own_right(g).wait_recv()
            cross_to_left(g).start()

        @pl.when(cross_right)
        def _():
            own_left(g).wait_recv()
            cross_to_right(g).start()

        @pl.when(jnp.logical_and(crosses, g < chunks - 2))
        def _():
            @pl.when(g < chunks - 3)
            def _():
                send_edges(g + 3)

            send_middle(g + 2)

    def compute(g):
        to_partner(g, 2).wait_recv()

        @pl.when(jnp.logical_and(has_left, jnp.logical_not(cross_left)))
        def _():
            own_right(g).wait_recv()

        @pl.when(jnp.logical_and(has_right, jnp.logical_not(cross_right)))
        def _():
            own_left(g).wait_recv()

        @pl.when(has_left)
        def _():
            relay_right(g).wait_recv()

        @pl.when(has_right)
        def _():
            relay_left(g).wait_recv()

        for head in range(PAIR):
            attend(pl.ds(pl.multiple_of(g * wide + head * HD, HD), HD))

    lag = jnp.where(crosses, 2, 1)
    shift = jnp.where(z < 2, 2, jnp.where(z < n_z // 2, 1, 0))
    shift = jnp.where(tm + h + z == 0, 0, shift)

    def chunk(g, carry):
        @pl.when(g < chunks)
        def _():
            forward(g)

        for stage in range(hops + 1):

            @pl.when(g == stage + shift)
            def _():
                ring_stage(stage)

        @pl.when(jnp.logical_and(g >= lag, g < chunks + lag))
        def _():
            compute(g - lag)

        return carry

    lax.fori_loop(0, chunks + 2, chunk, 0)

    step_load.wait()
    for copy in gate_loads:
        copy.wait()
    for offset in range(n_z):
        across(offset).wait_recv()

    which = step_now[0]
    gate_row = gates[0, pl.ds(which, 1), :]
    slope_row = gates[1, pl.ds(which, 1), :]
    span = n_z * shard
    for height in range(n_h):
        outs = slice(height * span, (height + 1) * span)
        both = None
        for part in range(2):
            weight = jnp.concatenate(
                [wbuf[part, i, height * shard : (height + 1) * shard, :] for i in range(n_z)], 0
            )
            term = lax.dot_general(
                attn[:, part * khalf : (part + 1) * khalf],
                weight,
                NT,
                preferred_element_type=jnp.float32,
            )
            both = term if both is None else both + term
        gate = gate_row[:, outs]
        outp_ref[:, outs] = (gate * both[:tokens]).astype(outp_ref.dtype)
        tangent = gate * both[tokens:] + slope_row[:, outs] * both[:tokens]
        outt_ref[:, outs] = tangent.astype(outt_ref.dtype)

    def finish(g, carry):
        for piece in range(3):
            to_partner(g, piece).wait_send()

        @pl.when(has_left)
        def _():
            own_left(g).wait_send()
            relay_left(g).wait_send()

        @pl.when(has_right)
        def _():
            own_right(g).wait_send()
            relay_right(g).wait_send()

        return carry

    lax.fori_loop(0, chunks, finish, 0)
    to_p.wait_send()
    to_g.wait_send()
    on_g.wait_send()
    for step in range(hops):
        for sub in range(2):
            if step < hops - 1 or sub == 0:
                ring_up(step, sub).wait_send()
            if step < hops - 1 or sub == 1:
                ring_down(step, sub).wait_send()
    for offset in range(n_z):
        across(offset).wait_send()


def local(sizes, q, k, v, qt, kt, vt, weight, gate_table, gate_slope, timestep):
    _, frames, rows, cols, features = q.shape
    tokens = frames * rows * cols
    frame = rows * cols
    shard = weight.shape[1]
    n_tm, n_h, n_z = sizes
    chunks = features // (PAIR * HD)
    flat = [pltpu.with_memory_space_constraint(a.reshape(tokens, features), pltpu.HBM) for a in (q, k, v, qt, kt, vt)]
    steps = gate_table.shape[0]
    dma = pltpu.SemaphoreType.DMA
    dims = (n_tm, n_h, n_z, tokens, frame, features, shard)
    weights = 3 + 2 * n_z + n_z
    anywhere = pl.BlockSpec(memory_space=pl.ANY)
    out = jax.ShapeDtypeStruct((tokens, features), jnp.bfloat16)
    out_p, out_t = pl.pallas_call(
        functools.partial(kernel, dims),
        out_shape=(out, out),
        in_specs=[pl.BlockSpec(memory_space=pltpu.HBM)] + [anywhere] * 9,
        out_specs=(pl.BlockSpec(memory_space=pltpu.VMEM),) * 2,
        scratch_shapes=[
            pltpu.VMEM((4, 2 * tokens + 4 * frame, features), jnp.bfloat16),
            pltpu.VMEM((2, tokens, features), jnp.bfloat16),
            pltpu.VMEM((2 * tokens, features), jnp.bfloat16),
            pltpu.VMEM((2, n_z, n_h * shard, features // 2), jnp.bfloat16),
            pltpu.VMEM((2, steps, features), jnp.float32),
            pltpu.SMEM((1,), jnp.int32),
            pltpu.SemaphoreType.REGULAR((6,)),
            dma((10,)),
        ]
        + [dma((3 * chunks,))] * 2
        + [dma((chunks,))] * 8
        + [dma((weights,))] * 2,
        compiler_params=pltpu.CompilerParams(vmem_limit_bytes=24 << 20, collective_id=0, has_side_effects=True),
        name="tiled_attention",
    )(timestep, *flat, *(pltpu.with_memory_space_constraint(a, pltpu.HBM) for a in (weight.T, gate_table, gate_slope)))
    return (out_p.reshape(q.shape), out_t.reshape(q.shape))


def solution(mesh):
    spec = P("fsdp", "tm", "height", None, None)
    in_specs = (spec,) * 6 + (P(None, ("height", "fsdp")), P(None, None), P(None, None), P("fsdp"))
    sizes = (mesh.shape["tm"], mesh.shape["height"], mesh.shape["fsdp"])
    return jax.shard_map(
        functools.partial(local, sizes),
        mesh=mesh,
        in_specs=in_specs,
        out_specs=(spec, spec),
        check_vma=False,
    )
```
